1024 devices in a mesh: dp: 16 (over z, core), expert: 64 (over y, x).
Axes of the slice: x: 8, y: 8, z: 8, core: 2. Of those that a mesh axis runs over, the one named last changes fastest.
Arguments:
- tokens: bfloat16 [131072, 3584], P(('dp', 'expert')), may hold values from -6 to 6
- expert_ids: int32 [131072, 1], P(('dp', 'expert')), may hold values from 0 to 63; in each aligned block of 128 rows (0 to 127, 128 to 255, ...) at most 4 rows name the same one
- gates: bfloat16 [131072], P(('dp', 'expert')), may hold values from 0.19921875 to 1
- cotangent: bfloat16 [131072, 1024], P(('dp', 'expert')), may hold values from -6 to 6
- weights: bfloat16 [64, 3584, 1024], P('expert'), may hold values from -0.09375 to 0.09375
Outputs:
- hidden: bfloat16 [131072, 1024], P(('dp', 'expert'))
- grad: float32 [64, 3584, 1024], P('expert', 'dp')
The draws below stay inside these ranges and needn't reach their ends.
Inputs may be any that keep to these rules, and one draw needn't show every extreme that they name: `expert_ids`: among the 128 tokens of one device at most 4 name one expert; some device and expert reach 4 in every draw.
All inputs are finite; a program needn't handle non-finite values.
Results may differ from the reference program's by a relative error of at most 0.0029.
Values may be sent and summed in bfloat16 or wider, within the bound.
A program may use at most 64 MiB of HBM per device.

```python
import math
import jax
import jax.numpy as jnp
import numpy as np
from jax import lax

D = 3584
H = 1024
TOK_DEV = 128
CAP = 4
EXPERTS = 64
TOKENS = 131072
N_DP = 16
N_EXPERT = 64


def shard_levels(own_key, dims, pieces, low, high):
    loudness, own = 1.0, jax.random.fold_in(own_key, 6)
    for axis_at, blocks in pieces:
        heights = jnp.exp(jax.random.uniform(jax.random.fold_in(own, axis_at), (blocks,), jnp.float32, low / len(pieces), high / len(pieces)))
        loudness = loudness * jnp.repeat(heights, dims[axis_at] // blocks).reshape([-1 if axis == axis_at else 1 for axis in range(len(dims))])
    return loudness


def assign_block(key, own, number, rows, count, top, reach, slope):
    sequence = jax.random.permutation(key, count)
    packed, usual = portions_of(count, rows * top, reach, slope, True), portions_of(count, rows * top, reach, slope, False)
    places = jnp.arange(count)

    def named(lengths, turn):
        used = int((lengths > 0).sum())
        fixed = max(1, used // 4)
        moved = fixed + (places - fixed + turn * (used - fixed)) % max(1, count - fixed)
        return jnp.zeros((count,), jnp.int32).at[sequence[jnp.where(places < fixed, places, moved)]].set(jnp.asarray(lengths, jnp.int32))

    lengths = jnp.where(number % 4 == 0, named(packed, number // 4), named(usual, number - number // 4 - 1))
    mixed = jax.random.permutation(jax.random.fold_in(own, 3), count)
    donor, sink = mixed[0:count // 2 * 2:2], mixed[1:count // 2 * 2:2]
    room = jnp.minimum(lengths[donor] - 1, reach - lengths[sink]) // 2
    room = jnp.where((donor == sequence[0]) | (sink == sequence[0]) | (lengths[sink] == 0), 0, jnp.maximum(room, 0))
    moved = jax.random.randint(jax.random.fold_in(own, 4), (count // 2,), 0, 1 << 20) % (room + 1)
    lengths = lengths.at[donor].add(-moved).at[sink].add(moved)
    labels = jnp.searchsorted(jnp.cumsum(lengths), jnp.arange(rows * top), side="right").astype(jnp.int32)
    grid = labels.reshape(top, rows).T
    grid = grid[jax.random.permutation(jax.random.fold_in(own, 1), rows)]
    turn = jax.random.randint(jax.random.fold_in(own, 2), (rows, 1), 0, top)
    return jnp.take_along_axis(grid, (jnp.arange(top)[None, :] + turn) % top, axis=1)


def portions_of(amount, total, limit, lean, full):
    portions = [(1 << 20) // math.isqrt(standing ** lean) + 1 for standing in range(1, amount + 1)]
    largest = limit if full else min(limit, max(-(-total // amount), total * portions[0] // sum(portions)))
    least = 1 if total - largest >= amount - 1 else 0
    given, rest = [largest] + [least] * (amount - 1), total - largest - least * (amount - 1)
    while rest > 0:
        free = [i for i in range(1, amount) if given[i] < largest] or [i for i in range(1, amount) if given[i] < limit]
        whole, budget = sum([portions[i] for i in free]), rest
        for i in free:
            addition = min(limit - given[i], max(1, budget * portions[i] // whole), rest)
            given[i] = given[i] + addition
            rest = rest - addition
    return np.array(given)


def gaussian(key, extent, spread, most, split=(), kind=jnp.bfloat16):
    values = spread * jax.random.normal(key, extent, jnp.float32)
    if split:
        values = values * shard_levels(key, extent, split, -0.22, 0.18)
    return jnp.clip(values, -most, most).astype(kind)


def setup_inputs(seed: int = 0) -> dict:
    streams_of = jax.random.split(jax.random.key(seed), 6)
    tokens = gaussian(streams_of[0], (TOKENS, D), 1.0, 6.0, ((0, 1024),))
    expert_ids_keys = jax.random.split(jax.random.fold_in(streams_of[1], 1), TOKENS // TOK_DEV)
    expert_ids_turns = jax.random.permutation(jax.random.fold_in(streams_of[1], 3), TOKENS // TOK_DEV)
    expert_ids = jax.vmap(lambda own, number: assign_block(jax.random.fold_in(streams_of[1], 2), own, number, TOK_DEV, EXPERTS, 1, CAP, 2))(expert_ids_keys, expert_ids_turns).reshape((TOKENS, 1))
    gates = jnp.clip(0.19921875 + 0.80078125 * jax.random.uniform(streams_of[2], (TOKENS,), jnp.float32) ** shard_levels(streams_of[2], (TOKENS,), ((0, 1024),), -0.2, 0.2), 0.19921875, 1.0).astype(jnp.bfloat16)
    cotangent = gaussian(streams_of[3], (TOKENS, H), 1.0, 6.0, ((0, 1024),))
    weights = gaussian(streams_of[4], (EXPERTS, D, H), D ** -0.5, 0.09375, ((0, 64),))
    return dict(tokens=tokens, expert_ids=expert_ids, gates=gates, cotangent=cotangent, weights=weights)


def reference(tokens, expert_ids, gates, cotangent, weights):
    ndev = TOKENS // TOK_DEV
    ids = expert_ids[:, 0].reshape(ndev, TOK_DEV)
    onehot = (ids[:, :, None] == jnp.arange(EXPERTS, dtype=jnp.int32)[None, None, :]).astype(jnp.int32)
    before = jnp.cumsum(onehot, axis=1) - onehot
    rank = jnp.sum(before * onehot, axis=2).astype(jnp.int32)
    device = jnp.broadcast_to(jnp.arange(ndev, dtype=jnp.int32)[:, None], (ndev, TOK_DEV))
    group = device // N_EXPERT
    source = device % N_EXPERT
    tok_index = jnp.arange(TOKENS, dtype=jnp.int32).reshape(ndev, TOK_DEV)
    table = jnp.full((N_DP, EXPERTS, N_EXPERT, CAP), -1, jnp.int32)
    table = table.at[group, ids, source, rank].set(tok_index)
    table = table.reshape(N_DP, EXPERTS, N_EXPERT * CAP)

    def per_expert(args):
        index, weight = args
        valid = index >= 0
        safe = jnp.where(valid, index, 0)
        rows = jnp.where(valid[:, None], tokens[safe], jnp.zeros((), jnp.bfloat16))
        gate = jnp.where(valid, gates[safe].astype(jnp.float32), 0.0)[:, None]
        cots = jnp.where(valid[:, None], cotangent[safe].astype(jnp.float32), 0.0)
        pre = jnp.dot(rows, weight, preferred_element_type=jnp.float32)
        sig = jax.nn.sigmoid(pre)
        hval = (gate * pre * sig).astype(jnp.bfloat16)
        dpre = (cots * gate * sig * (1.0 + pre * (1.0 - sig))).astype(jnp.bfloat16)
        part = jnp.dot(rows.T, dpre, preferred_element_type=jnp.float32)
        return hval, part

    def per_group(total, index):
        hvals, parts = lax.map(per_expert, (index, weights))
        return total + parts, hvals

    grad, hvals = lax.scan(per_group, jnp.zeros((EXPERTS, D, H), jnp.float32), table)
    flat = hvals.reshape(N_DP * EXPERTS * N_EXPERT * CAP, H)
    where = ((group * EXPERTS + ids) * N_EXPERT + source) * CAP + rank
    hidden = flat[where.reshape(TOKENS)]
    return hidden, grad
```

```python
import functools

import jax
import jax.numpy as jnp
from jax import lax
from jax.experimental import pallas as pl
from jax.experimental.pallas import tpu as pltpu
from jax.sharding import PartitionSpec as P

MESH = pl.DeviceIdType.MESH
LANES = 128
BF = jnp.bfloat16
F32 = jnp.float32


def aligned(start, size):
    return pl.ds(pl.multiple_of(start, size), size)


def kernel(
    cfg,
    ids_ref,
    gates_ref,
    tok_hbm,
    cot_hbm,
    w_hbm,
    hid_ref,
    grad_ref,
    tok,
    cot,
    w,
    xs,
    cs,
    xr,
    cr,
    xt,
    xtp,
    fac,
    dpre,
    dprep,
    hv,
    hr,
    sbuf,
    rbuf,
    spare,
    local_sem,
    x_sem,
    c_sem,
    h_sem,
    t_sem,
    d_sem,
    rs_send,
    rs_recv,
):
    experts, cap, side, ring = cfg
    rows = experts * cap
    tall = experts // side
    width, inner = w.shape
    count = tok.shape[0]
    share = grad_ref.shape[0]
    half = share // 2
    far = ring // 2
    steps = ring - 1

    dp = lax.axis_index("dp")
    me = lax.axis_index("expert")
    z, core = dp // 2, dp % 2
    my_y, my_x = me // side, me % side
    partner = 2 * z + 1 - core
    ahead = 2 * ((z + 1) % ring) + core
    behind = 2 * ((z + ring - 1) % ring) + core

    def zigzag(i, n):
        return jnp.where(i % 2 == 1, (i + 1) // 2, (n - i // 2) % n)

    def peer(k):
        py = (my_y + zigzag(k // side, tall)) % tall
        px = (my_x + zigzag(k % side, side)) % side
        return py * side + px

    load_tok = pltpu.make_async_copy(tok_hbm, tok, local_sem.at[0])
    load_cot = pltpu.make_async_copy(cot_hbm, cot, local_sem.at[1])
    load_w = pltpu.make_async_copy(w_hbm.at[0], w, local_sem.at[2])
    load_tok.start()
    load_cot.start()

    barrier = pltpu.get_barrier_semaphore()

    def greet(k, carry):
        pl.semaphore_signal(barrier, inc=1, device_id=(dp, peer(k)), device_id_type=MESH)
        return carry

    lax.fori_loop(1, experts, greet, 0)
    for other in (partner, ahead, behind):
        pl.semaphore_signal(barrier, inc=1, device_id=(other, me), device_id_type=MESH)
    load_w.start()

    mine = jnp.broadcast_to(ids_ref[...], (count, count))
    earlier = lax.broadcasted_iota(jnp.int32, (count, count), 0) < lax.broadcasted_iota(
        jnp.int32, (count, count), 1
    )
    same = jnp.where((mine == mine.T) & earlier, 1, 0)
    slot = ids_ref[...] * cap + jnp.sum(same, axis=0, keepdims=True)
    hot = lax.broadcasted_iota(jnp.int32, (rows, count), 0) == slot
    placing32 = jnp.where(hot, 1.0, 0.0).astype(F32)
    placing = placing32.astype(BF)
    gate_col = jnp.sum(placing32 * gates_ref[...].astype(F32), axis=1, keepdims=True)
    xs[:, width:] = jnp.broadcast_to(gate_col, (rows, LANES)).astype(BF)

    load_tok.wait()
    block = 512 if width % 512 == 0 else LANES

    def place_x(i, carry):
        cols = aligned(i * block, block)
        xs[:, cols] = jnp.dot(placing, tok[:, cols], preferred_element_type=F32).astype(BF)
        return carry

    lax.fori_loop(0, width // block, place_x, 0)
    pl.semaphore_wait(barrier, experts - 1 + 3)

    def send_all(src, dst, sem, n):
        def go(k, carry):
            to = peer(k)
            pltpu.make_async_remote_copy(
                src_ref=src.at[aligned(to * cap, cap)],
                dst_ref=dst.at[aligned(me * cap, cap)],
                send_sem=sem.at[0],
                recv_sem=sem.at[1],
                device_id=(dp, to),
                device_id_type=MESH,
            ).start()
            return carry

        lax.fori_loop(1, experts, go, 0)
        own = aligned(me * cap, cap)
        pltpu.make_async_copy(src.at[own], dst.at[own], sem.at[1]).start()
        pltpu.make_async_copy(src.at[own], spare.at[n, pl.ds(0, cap), pl.ds(0, src.shape[1])], sem.at[0]).start()

    def whole(src, dst, sem):
        return pltpu.make_async_remote_copy(
            src_ref=src,
            dst_ref=dst,
            send_sem=sem.at[0],
            recv_sem=sem.at[1],
            device_id=(dp, peer(1)),
            device_id_type=MESH,
        )

    send_all(xs, xr, x_sem, 0)
    load_cot.wait()
    cs[...] = jnp.dot(placing, cot[...], preferred_element_type=F32).astype(BF)
    send_all(cs, cr, c_sem, 1)

    load_w.wait()
    whole(xs, xr, x_sem).wait_recv()

    tb = 256 if width % 256 == 0 else LANES

    def turn(i, carry):
        cols = aligned(i * tb, tb)
        xt[cols, :] = xr[:, cols].T
        return carry

    lax.fori_loop(0, width // tb, turn, 0)
    swaps = []
    for j in range(ring):
        swap = pltpu.make_async_remote_copy(
            src_ref=xt.at[aligned((2 * j + 1 - core) * share, share)],
            dst_ref=xtp.at[pl.ds(j * share, share)],
            send_sem=t_sem.at[0, j],
            recv_sem=t_sem.at[1, j],
            device_id=(partner, me),
            device_id_type=MESH,
        )
        swap.start()
        swaps.append(swap)

    nb = min(256, inner)

    def forward(i, carry):
        cols = aligned(i * nb, nb)
        pre = jnp.dot(xr[:, :width], w[:, cols], preferred_element_type=F32)
        gate = jnp.concatenate([xr[:, width:].astype(F32)] * (nb // LANES), axis=1)
        sig = jax.nn.sigmoid(pre)
        hv[:, cols] = (gate * pre * sig).astype(BF)
        fac[:, cols] = gate * sig * (1.0 + pre * (1.0 - sig))
        return carry

    lax.fori_loop(0, inner // nb, forward, 0)
    send_all(hv, hr, h_sem, 2)

    whole(cs, cr, c_sem).wait_recv()

    def backward(i, carry):
        cols = aligned(i * nb, nb)
        dpre[:, cols] = (cr[:, cols].astype(F32) * fac[:, cols]).astype(BF)
        return carry

    lax.fori_loop(0, inner // nb, backward, 0)
    give = pltpu.make_async_remote_copy(
        src_ref=dpre,
        dst_ref=dprep,
        send_sem=d_sem.at[0],
        recv_sem=d_sem.at[1],
        device_id=(partner, me),
        device_id_type=MESH,
    )
    give.start()
    for swap in swaps:
        swap.wait_recv()
    give.wait_recv()

    def chunk(j, which):
        own = xt[aligned((2 * j + core) * share + which * half, half), :]
        other = xtp[aligned(j * share + which * half, half), :]
        return jnp.dot(own, dpre[...], preferred_element_type=F32) + jnp.dot(
            other, dprep[...], preferred_element_type=F32
        )

    def message(way, m):
        return pltpu.make_async_remote_copy(
            src_ref=sbuf.at[way, m],
            dst_ref=rbuf.at[way, m],
            send_sem=rs_send.at[way, m],
            recv_sem=rs_recv.at[way, m],
            device_id=(ahead if way == 0 else behind, me),
            device_id_type=MESH,
        )

    def target(way, m):
        dist = far - (m + 1) // 2
        return (z + dist) % ring if way == 0 else (z + ring - dist) % ring

    for m in range(2):
        for way in range(2):
            sbuf[way, m] = chunk(target(way, m), (m + way) % 2).astype(BF)
            message(way, m).start()

    def relay(m, carry):
        for way in range(2):
            term = chunk(target(way, m), (m + way) % 2)
            message(way, m - 2).wait_recv()
            sbuf[way, m] = (term + rbuf[way, m - 2].astype(F32)).astype(BF)
            message(way, m).start()
        return carry

    lax.fori_loop(2, steps, relay, 0)

    for which in range(2):
        grad_ref[pl.ds(which * half, half), :] = chunk(z, which)

    whole(hv, hr, h_sem).wait_recv()
    hid_ref[...] = lax.dot_general(
        placing, hr[...], (((0,), (0,)), ((), ())), preferred_element_type=F32
    ).astype(BF)

    for m in (steps - 2, steps - 1):
        for way in range(2):
            message(way, m).wait_recv()
            at = pl.ds((m + way) % 2 * half, half)
            grad_ref[at, :] += rbuf[way, m].astype(F32)

    whole(xs, xr, x_sem).wait_send()
    whole(cs, cr, c_sem).wait_send()
    whole(hv, hr, h_sem).wait_send()
    for swap in swaps:
        swap.wait_send()
    give.wait_send()

    def drain(m, carry):
        for way in range(2):
            message(way, m).wait_send()
        return carry

    lax.fori_loop(0, steps, drain, 0)


def solution(mesh):
    n_dp, experts = mesh.shape["dp"], mesh.shape["expert"]
    ring = n_dp // 2
    side = 1
    while (2 * side) * (2 * side) <= experts:
        side *= 2

    def on_device(tokens, expert_ids, gates, cotangent, weights):
        count, width = tokens.shape
        inner = cotangent.shape[1]
        cap = max(2, 2 * count // experts)
        rows = experts * cap
        share = width // n_dp
        steps = ring - 1
        vmem = pl.BlockSpec(memory_space=pltpu.VMEM)
        hbm = pl.BlockSpec(memory_space=pl.ANY)
        dma = pltpu.SemaphoreType.DMA
        hidden, grad = pl.pallas_call(
            functools.partial(kernel, (experts, cap, side, ring)),
            out_shape=(
                jax.ShapeDtypeStruct((count, inner), BF),
                jax.ShapeDtypeStruct((share, inner), F32),
            ),
            in_specs=[vmem, vmem, hbm, hbm, hbm],
            out_specs=(vmem, vmem),
            scratch_shapes=[
                pltpu.VMEM((count, width), BF),
                pltpu.VMEM((count, inner), BF),
                pltpu.VMEM((width, inner), BF),
                pltpu.VMEM((rows, width + LANES), BF),
                pltpu.VMEM((rows, inner), BF),
                pltpu.VMEM((rows, width + LANES), BF),
                pltpu.VMEM((rows, inner), BF),
                pltpu.VMEM((width, rows), BF),
                pltpu.VMEM((width // 2, rows), BF),
                pltpu.VMEM((rows, inner), F32),
                pltpu.VMEM((rows, inner), BF),
                pltpu.VMEM((rows, inner), BF),
                pltpu.VMEM((rows, inner), BF),
                pltpu.VMEM((rows, inner), BF),
                pltpu.VMEM((2, steps, share // 2, inner), BF),
                pltpu.VMEM((2, steps, share // 2, inner), BF),
                pltpu.VMEM((3, max(cap, 8), width + LANES), BF),
                dma((3,)),
                dma((2,)),
                dma((2,)),
                dma((2,)),
                dma((2, ring)),
                dma((2,)),
                dma((2, steps)),
                dma((2, steps)),
            ],
            compiler_params=pltpu.CompilerParams(
                collective_id=0, has_side_effects=True, vmem_limit_bytes=56 << 20
            ),
        )(expert_ids.reshape(1, count), gates.reshape(1, count), tokens, cotangent, weights)
        return hidden, grad[None]

    return jax.shard_map(
        on_device,
        mesh=mesh,
        in_specs=(
            P(("dp", "expert"), None),
            P(("dp", "expert"), None),
            P(("dp", "expert")),
            P(("dp", "expert"), None),
            P("expert", None, None),
        ),
        out_specs=(P(("dp", "expert"), None), P("expert", "dp", None)),
        check_vma=False,
    )
```

```python
import functools

import jax
import jax.numpy as jnp
from jax import lax
from jax.experimental import pallas as pl
from jax.experimental.pallas import tpu as pltpu
from jax.sharding import PartitionSpec as P

MESH = pl.DeviceIdType.MESH
LANES = 128
BF = jnp.bfloat16
F32 = jnp.float32


def aligned(start, size):
    return pl.ds(pl.multiple_of(start, size), size)


def kernel(
    cfg,
    ids_ref,
    gates_ref,
    tok_hbm,
    cot_hbm,
    w_hbm,
    hid_ref,
    grad_ref,
    tok,
    cot,
    w,
    first,
    middle,
    last,
    h_first,
    h_middle,
    h_last,
    xt,
    xtp,
    fac,
    dpre,
    dprep,
    sbuf,
    rbuf,
    local_sem,
    own_sem,
    hop_send,
    hop_recv,
    t_sem,
    d_sem,
    rs_send,
    rs_recv,
):
    cap, side, tall, ring, slices, pieces = cfg
    rows = tall * side * cap
    width, inner = w.shape
    count = tok.shape[0]
    share = grad_ref.shape[0]
    half = share // 2
    far = ring // 2
    steps = ring - 1
    part = inner // slices
    n_x = len(pieces) - slices

    dp = lax.axis_index("dp")
    me = lax.axis_index("expert")
    z, core = dp // 2, dp % 2
    my_y, my_x = me // side, me % side
    partner = 2 * z + 1 - core
    ahead = 2 * ((z + 1) % ring) + core
    behind = 2 * ((z + ring - 1) % ring) + core

    def zigzag(i, n):
        return jnp.where(i % 2 == 1, (i + 1) // 2, (n - i // 2) % n)

    def y_peer(k):
        return (my_y + zigzag(k, tall)) % tall

    def x_peer(k):
        return (my_x + zigzag(k, side)) % side

    load_tok = pltpu.make_async_copy(tok_hbm, tok, local_sem.at[0])
    load_cot = pltpu.make_async_copy(cot_hbm, cot, local_sem.at[1])
    load_w = pltpu.make_async_copy(w_hbm.at[0], w, local_sem.at[2])
    load_tok.start()
    load_cot.start()

    barrier = pltpu.get_barrier_semaphore()

    def greet(to_dp, to):
        pl.semaphore_signal(barrier, inc=1, device_id=(to_dp, to), device_id_type=MESH)

    def greet_y(k, carry):
        greet(dp, y_peer(k) * side + my_x)
        return carry

    def greet_x(k, carry):
        greet(dp, my_y * side + x_peer(k))
        return carry

    lax.fori_loop(1, tall, greet_y, 0)
    lax.fori_loop(1, side, greet_x, 0)
    for other in (partner, ahead, behind):
        greet(other, me)
    load_w.start()

    mine = jnp.broadcast_to(ids_ref[...], (count, count))
    earlier = lax.broadcasted_iota(jnp.int32, (count, count), 0) < lax.broadcasted_iota(
        jnp.int32, (count, count), 1
    )
    same = jnp.where((mine == mine.T) & earlier, 1, 0)
    slot = ids_ref[...] * cap + jnp.sum(same, axis=0, keepdims=True)
    hot = lax.broadcasted_iota(jnp.int32, (rows, count), 0) == slot
    placing32 = jnp.where(hot, 1.0, 0.0).astype(F32)
    placing = placing32.astype(BF)

    def folded(v):
        return v.reshape(tall, side * cap, v.shape[1])

    def flat(ref, start, size):
        return ref[:, :, start : start + size].reshape(rows, size)

    def placed(source, start, size):
        return folded(
            jnp.dot(placing, source[:, start : start + size], preferred_element_type=F32).astype(BF)
        )

    def place(p):
        start, size = pieces[p][0], pieces[p][1] + pieces[p][2]
        if p >= n_x:
            first[:, :, start : start + size] = placed(cot, start - width - LANES, size)
            return
        here = min(size, width - start)
        first[:, :, start : start + here] = placed(tok, start, here)
        if here < size:
            gate_col = jnp.sum(placing32 * gates_ref[...].astype(F32), axis=1, keepdims=True)
            first[:, :, width : width + LANES] = folded(
                jnp.broadcast_to(gate_col, (rows, LANES)).astype(BF)
            )

    def hop(src, dst, p, hopno, which, cols):
        def copy(s, d, to):
            pltpu.make_async_remote_copy(
                src_ref=s,
                dst_ref=d,
                send_sem=hop_send.at[p, hopno, which],
                recv_sem=hop_recv.at[p, hopno, which],
                device_id=(dp, to),
                device_id_type=MESH,
            ).start()

        if hopno == which:

            def go(k, carry):
                to = y_peer(k)
                copy(src.at[to, :, cols], dst.at[my_y, :, cols], to * side + my_x)
                return carry

            lax.fori_loop(1, tall, go, 0)
        else:
            mine4 = aligned(my_x * cap, cap)

            def go(k, carry):
                to = x_peer(k)
                copy(
                    src.at[:, aligned(to * cap, cap), cols],
                    dst.at[:, mine4, cols],
                    my_y * side + to,
                )
                return carry

            lax.fori_loop(1, side, go, 0)
        own_copy(src, dst, p, hopno, which, cols).start()

    def own_copy(src, dst, p, hopno, which, cols):
        if hopno == which:
            s, d = src.at[my_y, :, cols], dst.at[my_y, :, cols]
        else:
            mine4 = aligned(my_x * cap, cap)
            s, d = src.at[:, mine4, cols], dst.at[:, mine4, cols]
        return pltpu.make_async_copy(s, d, own_sem.at[p, hopno, which])

    def others(src, dst, p, hopno, which, cols):
        n = tall - 1 if hopno == which else tall * (side - 1) // side
        return pltpu.make_async_remote_copy(
            src_ref=src.at[pl.ds(0, n), :, cols],
            dst_ref=dst.at[pl.ds(0, n), :, cols],
            send_sem=hop_send.at[p, hopno, which],
            recv_sem=hop_recv.at[p, hopno, which],
            device_id=(ahead, me),
            device_id_type=MESH,
        )

    def bufs(p, hopno):
        chain = (first, middle, last) if p < len(pieces) else (h_first, h_middle, h_last)
        return chain[hopno], chain[hopno + 1]

    def blocks(p):
        start, a, b = pieces[p] if p < len(pieces) else (0, inner // 2, inner // 2)
        return ((0, pl.ds(start, a)), (1, pl.ds(start + a, b)))

    def send_piece(p, hopno):
        src, dst = bufs(p, hopno)
        for which, cols in blocks(p):
            hop(src, dst, p, hopno, which, cols)

    def await_piece(p, hopno):
        src, dst = bufs(p, hopno)
        for which, cols in blocks(p):
            own_copy(src, dst, p, hopno, which, cols).wait()
            others(src, dst, p, hopno, which, cols).wait_recv()

    nb = min(256, part)

    def swap(j):
        return pltpu.make_async_remote_copy(
            src_ref=xt.at[aligned((2 * j + 1 - core) * share, share)],
            dst_ref=xtp.at[pl.ds(j * share, share)],
            send_sem=t_sem.at[0, j],
            recv_sem=t_sem.at[1, j],
            device_id=(partner, me),
            device_id_type=MESH,
        )

    def forward(p):
        start = pieces[p][0]
        size = min(pieces[p][1] + pieces[p][2], width - start)
        tb = 256 if size % 256 == 0 else LANES
        for i in range(size // tb):
            at = start + i * tb
            xt[pl.ds(at, tb), :] = flat(last, at, tb).T
        if p == n_x - 1:
            for j in range(ring):
                swap(j).start()

        def one(i, carry):
            cols = aligned(i * nb, nb)
            pre = jnp.dot(
                flat(last, start, size), w[start : start + size, cols], preferred_element_type=F32
            )
            if p > 0:
                pre = pre + fac[:, cols]
            if p < n_x - 1:
                fac[:, cols] = pre
                return carry
            gate = jnp.concatenate([flat(last, width, LANES).astype(F32)] * (nb // LANES), axis=1)
            sig = jax.nn.sigmoid(pre)
            h_first[:, :, cols] = folded((gate * pre * sig).astype(BF))
            fac[:, cols] = gate * sig * (1.0 + pre * (1.0 - sig))
            return carry

        lax.fori_loop(0, inner // nb, one, 0)

    def give(hs):
        return pltpu.make_async_remote_copy(
            src_ref=dpre.at[hs],
            dst_ref=dprep.at[hs],
            send_sem=d_sem.at[0, hs],
            recv_sem=d_sem.at[1, hs],
            device_id=(partner, me),
            device_id_type=MESH,
        )

    def chunk(j, which, hs):
        own = xt[aligned((2 * j + core) * share + which * half, half), :]
        other = xtp[aligned(j * share + which * half, half), :]
        return jnp.dot(own, dpre[hs], preferred_element_type=F32) + jnp.dot(
            other, dprep[hs], preferred_element_type=F32
        )

    def message(way, hs, m):
        return pltpu.make_async_remote_copy(
            src_ref=sbuf.at[way, hs, m],
            dst_ref=rbuf.at[way, hs, m],
            send_sem=rs_send.at[way, hs, m],
            recv_sem=rs_recv.at[way, hs, m],
            device_id=(ahead if way == 0 else behind, me),
            device_id_type=MESH,
        )

    def target(way, m):
        dist = far - (m + 1) // 2
        return (z + dist) % ring if way == 0 else (z + ring - dist) % ring

    def backward(hs):
        for i in range(part // nb):
            at = hs * part + i * nb
            dpre[hs, :, i * nb : (i + 1) * nb] = (
                flat(last, width + LANES + at, nb).astype(F32) * fac[:, at : at + nb]
            ).astype(BF)
        give(hs).start()
        if hs == 0:
            for j in range(ring):
                swap(j).wait_recv()
        give(hs).wait_recv()
        for m in range(2):
            for way in range(2):
                sbuf[way, hs, m] = chunk(target(way, m), (m + way) % 2, hs).astype(BF)
                message(way, hs, m).start()

    load_tok.wait()
    place(0)
    pl.semaphore_wait(barrier, tall - 1 + side - 1 + 3)
    send_piece(0, 0)
    n_p = len(pieces)
    place(1)
    send_piece(1, 0)
    load_cot.wait()
    for p in range(2, n_p):
        place(p)
    load_w.wait()

    def work(p):
        await_piece(p, 1)
        if p < n_x:
            forward(p)
        else:
            backward(p - n_x)

    for p in range(n_p):
        await_piece(p, 0)
        send_piece(p, 1)
        if p + 2 < n_p:
            send_piece(p + 2, 0)
        if p == n_p - 1:
            send_piece(n_p, 0)
        if p > 0:
            work(p - 1)
    work(n_p - 1)

    def relay(m, carry):
        for hs in range(slices):
            for way in range(2):
                term = chunk(target(way, m), (m + way) % 2, hs)
                message(way, hs, m - 2).wait_recv()
                sbuf[way, hs, m] = (term + rbuf[way, hs, m - 2].astype(F32)).astype(BF)
                message(way, hs, m).start()
        return carry

    relay(2, 0)
    await_piece(n_p, 0)
    send_piece(n_p, 1)
    lax.fori_loop(3, steps, relay, 0)

    for which in range(2):
        for hs in range(slices):
            grad_ref[pl.ds(which * half, half), pl.ds(hs * part, part)] = chunk(z, which, hs)

    await_piece(n_p, 1)
    hid_ref[...] = lax.dot_general(
        placing, flat(h_last, 0, inner), (((0,), (0,)), ((), ())), preferred_element_type=F32
    ).astype(BF)

    for m in (steps - 2, steps - 1):
        for hs in range(slices):
            for way in range(2):
                message(way, hs, m).wait_recv()
                at = pl.ds((m + way) % 2 * half, half)
                grad_ref[at, pl.ds(hs * part, part)] += rbuf[way, hs, m].astype(F32)

    for p in range(n_p + 1):
        for hopno in range(2):
            src, dst = bufs(p, hopno)
            for which, cols in blocks(p):
                others(src, dst, p, hopno, which, cols).wait_send()
    for j in range(ring):
        swap(j).wait_send()
    for hs in range(slices):
        give(hs).wait_send()

    def drain(m, carry):
        for hs in range(slices):
            for way in range(2):
                message(way, hs, m).wait_send()
        return carry

    lax.fori_loop(0, steps, drain, 0)


def solution(mesh):
    n_dp, experts = mesh.shape["dp"], mesh.shape["expert"]
    ring = n_dp // 2
    side = 1
    while (2 * side) * (2 * side) <= experts:
        side *= 2
    tall = experts // side

    def on_device(tokens, expert_ids, gates, cotangent, weights):
        count, width = tokens.shape
        inner = cotangent.shape[1]
        cap = max(2, 2 * count // experts)
        rows = experts * cap
        share = width // n_dp
        steps = ring - 1
        slices = 2
        part = inner // slices
        pieces, at = [], 0
        while width - at >= 8 * LANES:
            pieces.append((at, 4 * LANES, 4 * LANES))
            at += 8 * LANES
        tiles = (width - at) // LANES + 1
        pieces.append((at, tiles // 2 * LANES, (tiles - tiles // 2) * LANES))
        for hs in range(slices):
            pieces.append((width + LANES + hs * part, part // 2, part // 2))
        cols = width + LANES + inner
        vmem = pl.BlockSpec(memory_space=pltpu.VMEM)
        hbm = pl.BlockSpec(memory_space=pl.ANY)
        dma = pltpu.SemaphoreType.DMA
        hidden, grad = pl.pallas_call(
            functools.partial(kernel, (cap, side, tall, ring, slices, tuple(pieces))),
            out_shape=(
                jax.ShapeDtypeStruct((count, inner), BF),
                jax.ShapeDtypeStruct((share, inner), F32),
            ),
            in_specs=[vmem, vmem, hbm, hbm, hbm],
            out_specs=(vmem, vmem),
            scratch_shapes=[
                pltpu.VMEM((count, width), BF),
                pltpu.VMEM((count, inner), BF),
                pltpu.VMEM((width, inner), BF),
                pltpu.VMEM((tall, side * cap, cols), BF),
                pltpu.VMEM((tall, side * cap, cols), BF),
                pltpu.VMEM((tall, side * cap, cols), BF),
                pltpu.VMEM((tall, side * cap, inner), BF),
                pltpu.VMEM((tall, side * cap, inner), BF),
                pltpu.VMEM((tall, side * cap, inner), BF),
                pltpu.VMEM((width, rows), BF),
                pltpu.VMEM((width // 2, rows), BF),
                pltpu.VMEM((rows, inner), F32),
                pltpu.VMEM((slices, rows, part), BF),
                pltpu.VMEM((slices, rows, part), BF),
                pltpu.VMEM((2, slices, steps, share // 2, part), BF),
                pltpu.VMEM((2, slices, steps, share // 2, part), BF),
                dma((3,)),
                dma((len(pieces) + 1, 2, 2)),
                dma((len(pieces) + 1, 2, 2)),
                dma((len(pieces) + 1, 2, 2)),
                dma((2, ring)),
                dma((2, slices)),
                dma((2, slices, steps)),
                dma((2, slices, steps)),
            ],
            compiler_params=pltpu.CompilerParams(
                collective_id=0, has_side_effects=True, vmem_limit_bytes=56 << 20
            ),
        )(expert_ids.reshape(1, count), gates.reshape(1, count), tokens, cotangent, weights)
        return hidden, grad[None]

    return jax.shard_map(
        on_device,
        mesh=mesh,
        in_specs=(
            P(("dp", "expert"), None),
            P(("dp", "expert"), None),
            P(("dp", "expert")),
            P(("dp", "expert"), None),
            P("expert", None, None),
        ),
        out_specs=(P(("dp", "expert"), None), P("expert", "dp", None)),
        check_vma=False,
    )
```

```python
import functools

import jax
import jax.numpy as jnp
from jax import lax
from jax.experimental import pallas as pl
from jax.experimental.pallas import tpu as pltpu
from jax.sharding import PartitionSpec as P

MESH = pl.DeviceIdType.MESH
LANES = 128
BF = jnp.bfloat16
F32 = jnp.float32


def aligned(start, size):
    return pl.ds(pl.multiple_of(start, size), size)


def kernel(
    cfg,
    ids_hbm,
    gates_hbm,
    tok_hbm,
    cot_hbm,
    w_hbm,
    hid_ref,
    grad_ref,
    ids_ref,
    gates_ref,
    tok,
    cot,
    w,
    first,
    middle,
    last,
    h_first,
    h_middle,
    h_last,
    xt,
    xtp,
    fac,
    dpre,
    dprep,
    sbuf,
    rbuf,
    local_sem,
    own_sem,
    hop_send,
    hop_recv,
    t_sem,
    d_sem,
    rs_send,
    rs_recv,
):
    cap, side, tall, ring, slices, pieces = cfg
    rows = tall * side * cap
    width, inner = w.shape
    count = tok.shape[0]
    share = grad_ref.shape[0]
    half = share // 2
    far = ring // 2
    steps = ring - 1
    part = inner // slices
    n_x = len(pieces) - slices

    dp = lax.axis_index("dp")
    me = lax.axis_index("expert")
    z, core = dp // 2, dp % 2
    my_y, my_x = me // side, me % side
    partner = 2 * z + 1 - core
    ahead = 2 * ((z + 1) % ring) + core
    behind = 2 * ((z + ring - 1) % ring) + core

    def offset(i, n):
        return jnp.where(i % 2 == 1, n - n // 2 - i // 2, n // 2 + i // 2)

    def y_peer(k):
        return (my_y + offset(k, tall)) % tall

    def x_peer(k):
        return (my_x + offset(k, side)) % side

    load_tok = pltpu.make_async_copy(tok_hbm, tok, local_sem.at[0])
    load_cot = pltpu.make_async_copy(cot_hbm, cot, local_sem.at[1])
    load_w = pltpu.make_async_copy(w_hbm.at[0], w, local_sem.at[2])
    load_ids = pltpu.make_async_copy(ids_hbm, ids_ref, local_sem.at[3])
    load_gates = pltpu.make_async_copy(gates_hbm, gates_ref, local_sem.at[4])
    for load in (load_ids, load_gates, load_tok, load_cot):
        load.start()

    barrier = pltpu.get_barrier_semaphore()

    def greet(to_dp, to):
        pl.semaphore_signal(barrier, inc=1, device_id=(to_dp, to), device_id_type=MESH)

    def greet_y(k, carry):
        greet(dp, y_peer(k) * side + my_x)
        return carry

    def greet_x(k, carry):
        greet(dp, my_y * side + x_peer(k))
        return carry

    lax.fori_loop(1, tall, greet_y, 0)
    lax.fori_loop(1, side, greet_x, 0)
    for other in (partner, ahead, behind):
        greet(other, me)
    load_w.start()

    load_ids.wait()
    load_gates.wait()
    mine = jnp.broadcast_to(ids_ref[...], (count, count))
    earlier = lax.broadcasted_iota(jnp.int32, (count, count), 0) < lax.broadcasted_iota(
        jnp.int32, (count, count), 1
    )
    same = jnp.where((mine == mine.T) & earlier, 1, 0)
    slot = ids_ref[...] * cap + jnp.sum(same, axis=0, keepdims=True)
    hot = lax.broadcasted_iota(jnp.int32, (rows, count), 0) == slot
    placing32 = jnp.where(hot, 1.0, 0.0).astype(F32)
    placing = placing32.astype(BF)

    def folded(v):
        return v.reshape(tall, side * cap, v.shape[1])

    def flat(ref, start, size):
        return ref[:, :, start : start + size].reshape(rows, size)

    def placed(source, start, size):
        return folded(
            jnp.dot(placing, source[:, start : start + size], preferred_element_type=F32).astype(BF)
        )

    def place(p):
        start, size = pieces[p][0], pieces[p][1] + pieces[p][2]
        if p >= n_x:
            first[:, :, start : start + size] = placed(cot, start - width - LANES, size)
            return
        here = min(size, width - start)
        first[:, :, start : start + here] = placed(tok, start, here)
        if here < size:
            gate_col = jnp.sum(placing32 * gates_ref[...].astype(F32), axis=1, keepdims=True)
            first[:, :, width : width + LANES] = folded(
                jnp.broadcast_to(gate_col, (rows, LANES)).astype(BF)
            )

    def hop(src, dst, p, hopno, which, cols):
        def copy(s, d, to):
            pltpu.make_async_remote_copy(
                src_ref=s,
                dst_ref=d,
                send_sem=hop_send.at[p, hopno, which],
                recv_sem=hop_recv.at[p, hopno, which],
                device_id=(dp, to),
                device_id_type=MESH,
            ).start()

        if hopno == which:

            def go(k, carry):
                to = y_peer(k)
                copy(src.at[to, :, cols], dst.at[my_y, :, cols], to * side + my_x)
                return carry

            lax.fori_loop(1, tall, go, 0)
        else:
            mine4 = aligned(my_x * cap, cap)

            def go(k, carry):
                to = x_peer(k)
                copy(
                    src.at[:, aligned(to * cap, cap), cols],
                    dst.at[:, mine4, cols],
                    my_y * side + to,
                )
                return carry

            lax.fori_loop(1, side, go, 0)
        own_copy(src, dst, p, hopno, which, cols).start()

    def own_copy(src, dst, p, hopno, which, cols):
        if hopno == which:
            s, d = src.at[my_y, :, cols], dst.at[my_y, :, cols]
        else:
            mine4 = aligned(my_x * cap, cap)
            s, d = src.at[:, mine4, cols], dst.at[:, mine4, cols]
        return pltpu.make_async_copy(s, d, own_sem.at[p, hopno, which])

    def others(src, dst, p, hopno, which, cols):
        n = tall - 1 if hopno == which else tall * (side - 1) // side
        return pltpu.make_async_remote_copy(
            src_ref=src.at[pl.ds(0, n), :, cols],
            dst_ref=dst.at[pl.ds(0, n), :, cols],
            send_sem=hop_send.at[p, hopno, which],
            recv_sem=hop_recv.at[p, hopno, which],
            device_id=(ahead, me),
            device_id_type=MESH,
        )

    def bufs(p, hopno):
        chain = (first, middle, last) if p < len(pieces) else (h_first, h_middle, h_last)
        return chain[hopno], chain[hopno + 1]

    def blocks(p):
        start, a, b = pieces[p] if p < len(pieces) else (0, inner // 2, inner // 2)
        return ((0, pl.ds(start, a)), (1, pl.ds(start + a, b)))

    def send_piece(p, hopno):
        src, dst = bufs(p, hopno)
        for which, cols in blocks(p):
            hop(src, dst, p, hopno, which, cols)

    def await_piece(p, hopno):
        src, dst = bufs(p, hopno)
        for which, cols in blocks(p):
            own_copy(src, dst, p, hopno, which, cols).wait()
            others(src, dst, p, hopno, which, cols).wait_recv()

    nb = min(256, part)

    def swap(j):
        return pltpu.make_async_remote_copy(
            src_ref=xt.at[aligned((2 * j + 1 - core) * share, share)],
            dst_ref=xtp.at[pl.ds(j * share, share)],
            send_sem=t_sem.at[0, j],
            recv_sem=t_sem.at[1, j],
            device_id=(partner, me),
            device_id_type=MESH,
        )

    def forward(p):
        start = pieces[p][0]
        size = min(pieces[p][1] + pieces[p][2], width - start)
        tb = 256 if size % 256 == 0 else LANES
        for i in range(size // tb):
            at = start + i * tb
            xt[pl.ds(at, tb), :] = flat(last, at, tb).T
        if p == n_x - 1:
            for j in range(ring):
                swap(j).start()

        def one(i, carry):
            cols = aligned(i * nb, nb)
            pre = jnp.dot(
                flat(last, start, size), w[start : start + size, cols], preferred_element_type=F32
            )
            if p > 0:
                pre = pre + fac[:, cols]
            if p < n_x - 1:
                fac[:, cols] = pre
                return carry
            gate = jnp.concatenate([flat(last, width, LANES).astype(F32)] * (nb // LANES), axis=1)
            sig = jax.nn.sigmoid(pre)
            h_first[:, :, cols] = folded((gate * pre * sig).astype(BF))
            fac[:, cols] = gate * sig * (1.0 + pre * (1.0 - sig))
            return carry

        lax.fori_loop(0, inner // nb, one, 0)

    def give(hs):
        return pltpu.make_async_remote_copy(
            src_ref=dpre.at[hs],
            dst_ref=dprep.at[hs],
            send_sem=d_sem.at[0, hs],
            recv_sem=d_sem.at[1, hs],
            device_id=(partner, me),
            device_id_type=MESH,
        )

    def chunk(j, which, hs):
        own = xt[aligned((2 * j + core) * share + which * half, half), :]
        other = xtp[aligned(j * share + which * half, half), :]
        return jnp.dot(own, dpre[hs], preferred_element_type=F32) + jnp.dot(
            other, dprep[hs], preferred_element_type=F32
        )

    def message(way, hs, m):
        return pltpu.make_async_remote_copy(
            src_ref=sbuf.at[way, hs, m],
            dst_ref=rbuf.at[way, hs, m],
            send_sem=rs_send.at[way, hs, m],
            recv_sem=rs_recv.at[way, hs, m],
            device_id=(ahead if way == 0 else behind, me),
            device_id_type=MESH,
        )

    def target(way, m):
        dist = far - (m + 1) // 2
        return (z + dist) % ring if way == 0 else (z + ring - dist) % ring

    def backward(hs):
        for i in range(part // nb):
            at = hs * part + i * nb
            dpre[hs, :, i * nb : (i + 1) * nb] = (
                flat(last, width + LANES + at, nb).astype(F32) * fac[:, at : at + nb]
            ).astype(BF)
        give(hs).start()
        if hs == 0:
            for j in range(ring):
                swap(j).wait_recv()
        give(hs).wait_recv()
        for m in range(2):
            for way in range(2):
                sbuf[way, hs, m] = chunk(target(way, m), (m + way) % 2, hs).astype(BF)
                message(way, hs, m).start()

    load_tok.wait()
    place(0)
    pl.semaphore_wait(barrier, tall - 1 + side - 1 + 3)
    send_piece(0, 0)
    n_p = len(pieces)
    place(1)
    send_piece(1, 0)
    load_cot.wait()
    for p in range(2, n_p):
        place(p)
    load_w.wait()

    def work(p):
        await_piece(p, 1)
        if p < n_x:
            forward(p)
        else:
            backward(p - n_x)

    for p in range(n_p):
        await_piece(p, 0)
        send_piece(p, 1)
        if p + 2 < n_p:
            send_piece(p + 2, 0)
        if p == n_p - 1:
            send_piece(n_p, 0)
        if p > 0:
            work(p - 1)
    work(n_p - 1)

    def relay(m, carry):
        for hs in range(slices):
            for way in range(2):
                term = chunk(target(way, m), (m + way) % 2, hs)
                message(way, hs, m - 2).wait_recv()
                sbuf[way, hs, m] = (term + rbuf[way, hs, m - 2].astype(F32)).astype(BF)
                message(way, hs, m).start()
        return carry

    relay(2, 0)
    await_piece(n_p, 0)
    send_piece(n_p, 1)
    lax.fori_loop(3, steps, relay, 0)

    for which in range(2):
        for hs in range(slices):
            grad_ref[pl.ds(which * half, half), pl.ds(hs * part, part)] = chunk(z, which, hs)

    await_piece(n_p, 1)
    hid_ref[...] = lax.dot_general(
        placing, flat(h_last, 0, inner), (((0,), (0,)), ((), ())), preferred_element_type=F32
    ).astype(BF)

    for m in (steps - 2, steps - 1):
        for hs in range(slices):
            for way in range(2):
                message(way, hs, m).wait_recv()
                at = pl.ds((m + way) % 2 * half, half)
                grad_ref[at, pl.ds(hs * part, part)] += rbuf[way, hs, m].astype(F32)

    for p in range(n_p + 1):
        for hopno in range(2):
            src, dst = bufs(p, hopno)
            for which, cols in blocks(p):
                others(src, dst, p, hopno, which, cols).wait_send()
    for j in range(ring):
        swap(j).wait_send()
    for hs in range(slices):
        give(hs).wait_send()

    def drain(m, carry):
        for hs in range(slices):
            for way in range(2):
                message(way, hs, m).wait_send()
        return carry

    lax.fori_loop(0, steps, drain, 0)


def deliver(hid, grad, hid_out, grad_out, sem):
    copies = [
        pltpu.make_async_copy(hid, hid_out, sem.at[0]),
        pltpu.make_async_copy(grad, grad_out, sem.at[1]),
    ]
    for copy in copies:
        copy.start()
    for copy in copies:
        copy.wait()


def solution(mesh):
    n_dp, experts = mesh.shape["dp"], mesh.shape["expert"]
    ring = n_dp // 2
    side = 1
    while (2 * side) * (2 * side) <= experts:
        side *= 2
    tall = experts // side

    def on_device(tokens, expert_ids, gates, cotangent, weights):
        count, width = tokens.shape
        inner = cotangent.shape[1]
        cap = max(2, 2 * count // experts)
        rows = experts * cap
        share = width // n_dp
        steps = ring - 1
        slices = 4
        part = inner // slices
        pieces, at = [], 0
        while width - at >= 8 * LANES:
            pieces.append((at, 4 * LANES, 4 * LANES))
            at += 8 * LANES
        tiles = (width - at) // LANES + 1
        pieces.append((at, tiles // 2 * LANES, (tiles - tiles // 2) * LANES))
        for hs in range(slices):
            pieces.append((width + LANES + hs * part, part // 2, part // 2))
        cols = width + LANES + inner
        vmem = pl.BlockSpec(memory_space=pltpu.VMEM)
        hbm = pl.BlockSpec(memory_space=pltpu.HBM)
        anywhere = pl.BlockSpec(memory_space=pl.ANY)
        dma = pltpu.SemaphoreType.DMA
        hidden, grad = pl.pallas_call(
            functools.partial(kernel, (cap, side, tall, ring, slices, tuple(pieces))),
            out_shape=(
                jax.ShapeDtypeStruct((count, inner), BF),
                jax.ShapeDtypeStruct((share, inner), F32),
            ),
            in_specs=[hbm] * 5,
            out_specs=(vmem, vmem),
            scratch_shapes=[
                pltpu.VMEM((1, count), jnp.int32),
                pltpu.VMEM((1, count), BF),
                pltpu.VMEM((count, width), BF),
                pltpu.VMEM((count, inner), BF),
                pltpu.VMEM((width, inner), BF),
                pltpu.VMEM((tall, side * cap, cols), BF),
                pltpu.VMEM((tall, side * cap, cols), BF),
                pltpu.VMEM((tall, side * cap, cols), BF),
                pltpu.VMEM((tall, side * cap, inner), BF),
                pltpu.VMEM((tall, side * cap, inner), BF),
                pltpu.VMEM((tall, side * cap, inner), BF),
                pltpu.VMEM((width, rows), BF),
                pltpu.VMEM((width // 2, rows), BF),
                pltpu.VMEM((rows, inner), F32),
                pltpu.VMEM((slices, rows, part), BF),
                pltpu.VMEM((slices, rows, part), BF),
                pltpu.VMEM((2, slices, steps, share // 2, part), BF),
                pltpu.VMEM((2, slices, steps, share // 2, part), BF),
                dma((5,)),
                dma((len(pieces) + 1, 2, 2)),
                dma((len(pieces) + 1, 2, 2)),
                dma((len(pieces) + 1, 2, 2)),
                dma((2, ring)),
                dma((2, slices)),
                dma((2, slices, steps)),
                dma((2, slices, steps)),
            ],
            compiler_params=pltpu.CompilerParams(
                collective_id=0, has_side_effects=True, vmem_limit_bytes=44 << 20
            ),
        )(
            *[
                pltpu.with_memory_space_constraint(v, pltpu.HBM)
                for v in (
                    expert_ids.reshape(1, count),
                    gates.reshape(1, count),
                    tokens,
                    cotangent,
                    weights,
                )
            ]
        )
        hidden, grad = pl.pallas_call(
            deliver,
            out_shape=(
                jax.ShapeDtypeStruct(hidden.shape, hidden.dtype),
                jax.ShapeDtypeStruct(grad.shape, grad.dtype),
            ),
            in_specs=[anywhere, anywhere],
            out_specs=(hbm, hbm),
            scratch_shapes=[dma((2,))],
            compiler_params=pltpu.CompilerParams(vmem_limit_bytes=1 << 20),
        )(hidden, grad)
        return hidden, grad[None]

    return jax.shard_map(
        on_device,
        mesh=mesh,
        in_specs=(
            P(("dp", "expert"), None),
            P(("dp", "expert"), None),
            P(("dp", "expert")),
            P(("dp", "expert"), None),
            P("expert", None, None),
        ),
        out_specs=(P(("dp", "expert"), None), P("expert", "dp", None)),
        check_vma=False,
    )
```
